256 devices in a mesh: grp: 16 (over z, core), clu: 16 (over y, x).
Axes of the slice: x: 4, y: 4, z: 8, core: 2. Of those that a mesh axis runs over, the one named last changes fastest.
Arguments:
- strengths: bfloat16 [32768, 128], P(('grp', 'clu')), may hold values from -6 to 6
- adjoint_weights: bfloat16 [32768, 128], P(('grp', 'clu')), may hold values from -6 to 6
- kernels: bfloat16 [49152, 2, 128, 128], P(('grp', 'clu')), may hold values from -0.02734375 to 0.02734375
- target_ids: int32 [49152], P(('grp', 'clu')), may hold values from 0 to 255, as said below
- source_ids: int32 [49152], P(('grp', 'clu')), may hold values from 0 to 255, as said below
- live_slots: int32 [256], P(('grp', 'clu')), may hold values from 48 to 192, as said below
Outputs:
- potential: float32 [32768, 128], P(('grp', 'clu'))
- adjoint_field: float32 [32768, 128], P(('grp', 'clu'))
The draws below stay inside these ranges and needn't reach their ends.
Inputs may be any that keep to these rules, and one draw needn't show every extreme that they name: `target_ids`: a slot's target block is one of the 16 blocks owned by the devices with the slot's grp index. `source_ids`: a slot's source block is owned by a device whose grp index equals that of the slot's device or differs from it by one. `live_slots`: some device uses all 192 slots.
All inputs are finite; a program needn't handle non-finite values.
Results may differ from the reference program's by a relative error of at most 0.0003.
Values may be sent and summed in bfloat16 or wider, within the bound.
A program may use at most 128 MiB of HBM per device.

```python
import jax
import jax.numpy as jnp
from jax import lax

PB = 128
BLK_DEV = 1
NNZ_DEV = 192
COLS = 128
GROUPS = 16
GROUP_BLOCKS = 16
NBLK = 256
NPANEL = 32768
SLOTS = 49152
N_CLU = 16
DEVICES = 256


def draw_target_ids(key, part):
    device = jnp.arange(SLOTS, dtype=jnp.int32) // NNZ_DEV
    group = device // N_CLU
    within = jax.random.randint(jax.random.fold_in(key, 11), (SLOTS,), 0, GROUP_BLOCKS)
    return (group * GROUP_BLOCKS + within).astype(jnp.int32)


def draw_source_ids(key, part):
    device = jnp.arange(SLOTS, dtype=jnp.int32) // NNZ_DEV
    group = device // N_CLU
    offset = jax.random.randint(jax.random.fold_in(key, 23), (SLOTS,), -1, 2)
    shifted = group + offset
    shifted = jnp.where((shifted < 0) | (shifted >= GROUPS), group, shifted)
    within = jax.random.randint(jax.random.fold_in(key, 29), (SLOTS,), 0, GROUP_BLOCKS)
    return (shifted * GROUP_BLOCKS + within).astype(jnp.int32)


def draw_live_slots(key, part):
    lowest = max(NNZ_DEV // 4, 1)
    counts = jax.random.randint(jax.random.fold_in(key, 31), (DEVICES,), lowest, NNZ_DEV + 1)
    fullest = jax.random.randint(jax.random.fold_in(key, 37), (), 0, DEVICES)
    return jnp.where(jnp.arange(DEVICES, dtype=jnp.int32) == fullest, NNZ_DEV, counts).astype(jnp.int32)


def levels(key, extent, cuts, smallest, top_value):
    loudness = 1.0
    for position, parts in cuts:
        heights = jax.random.uniform(jax.random.fold_in(jax.random.fold_in(key, 6), position), (parts,), jnp.float32, smallest / len(cuts), top_value / len(cuts))
        loudness = loudness * jnp.repeat(jnp.exp(heights), extent[position] // parts).reshape((-1,) + (1,) * (len(extent) - 1 - position))
    return loudness


def gaussian(rng, shape, scale, bound, shards=(), kind=jnp.bfloat16):
    level = levels(rng, shape, shards, -0.22, 0.18) if shards else 1.0
    values = jax.random.normal(rng, shape, jnp.float32) * scale * level
    return jnp.minimum(jnp.maximum(values, -bound), bound).astype(kind)


def setup_inputs(seed: int = 0) -> dict:
    key_of = jax.random.split(jax.random.key(seed), 7)
    return {
        "strengths": gaussian(key_of[0], (NPANEL, COLS), 1.0, 6.0, ((0, 256),)),
        "adjoint_weights": gaussian(key_of[1], (NPANEL, COLS), 1.0, 6.0, ((0, 256),)),
        "kernels": gaussian(key_of[2], (SLOTS, 2, PB, PB), (2 * PB * NNZ_DEV // BLK_DEV) ** -0.5, 0.02734375, ((0, 256),)),
        "target_ids": draw_target_ids(jax.random.fold_in(key_of[6], 71), 0),
        "source_ids": draw_source_ids(jax.random.fold_in(key_of[6], 71), 0),
        "live_slots": draw_live_slots(jax.random.fold_in(key_of[6], 71), 0),
    }


def complex_join(prod):
    half = prod.shape[-1] // 2
    real_part = prod[:, 0, :, :half] - prod[:, 1, :, half:]
    imag_part = prod[:, 0, :, half:] + prod[:, 1, :, :half]
    return jnp.concatenate([real_part, imag_part], axis=-1)


def reference(strengths, adjoint_weights, kernels, target_ids, source_ids, live_slots):
    sig_blocks = strengths.reshape(NBLK, PB, COLS).astype(jnp.float32)
    mu_blocks = adjoint_weights.reshape(NBLK, PB, COLS).astype(jnp.float32)
    kern = kernels.reshape(DEVICES, NNZ_DEV, 2, PB, PB)
    tgt = target_ids.reshape(DEVICES, NNZ_DEV)
    src = source_ids.reshape(DEVICES, NNZ_DEV)

    def step(carry, inputs):
        phi, psi = carry
        k_dev, t_dev, s_dev, count = inputs
        live = (jnp.arange(NNZ_DEV, dtype=jnp.int32) < count).astype(jnp.float32)[:, None, None]
        kf = k_dev.astype(jnp.float32)
        fwd = jnp.einsum('nkpq,nqc->nkpc', kf, sig_blocks[s_dev], precision=lax.Precision.HIGHEST)
        bwd = jnp.einsum('nkpq,npc->nkqc', kf, mu_blocks[t_dev], precision=lax.Precision.HIGHEST)
        phi = phi.at[t_dev].add(complex_join(fwd) * live)
        psi = psi.at[s_dev].add(complex_join(bwd) * live)
        return (phi, psi), None

    start = jnp.zeros((NBLK, PB, COLS), jnp.float32)
    (phi, psi), _ = lax.scan(step, (start, start), (kern, tgt, src, live_slots))
    return phi.reshape(NPANEL, COLS), psi.reshape(NPANEL, COLS)
```

```python
import functools

import jax
import jax.numpy as jnp
from jax import lax
from jax.experimental import pallas as pl
from jax.experimental.pallas import tpu as pltpu
from jax.sharding import PartitionSpec as P

MESH = pl.DeviceIdType.MESH
SIDE = 4
UNROLL = 8
REL = (2, 1, 3, 0)


class Links:
    def __init__(self, send, recv):
        self.send_sem, self.recv_sem, self.open = send, recv, []

    def make(self, index, src, dst, device):
        return pltpu.make_async_remote_copy(
            src_ref=src,
            dst_ref=dst,
            send_sem=self.send_sem.at[index],
            recv_sem=self.recv_sem.at[index],
            device_id=device,
            device_id_type=MESH,
        )

    def start(self, index, src, dst, device, when=None):
        copy = self.make(index, src, dst, device)
        if when is None:
            copy.start()
        else:
            pl.when(when)(copy.start)
        self.open.append((copy, when))

    def arrived(self, index, dst, device):
        self.make(index, dst, dst, device).wait_recv()

    def finish(self):
        for copy, when in self.open:
            if when is None:
                copy.wait_send()
            else:
                pl.when(when)(copy.wait_send)


def kernel(
    groups,
    s_ref,
    w_ref,
    tab_ref,
    k_hbm,
    pot_ref,
    adj_ref,
    kbuf,
    run_buf,
    s_all,
    s_two,
    w_all,
    w_two,
    padj,
    ppot,
    zin,
    relay_in,
    relay_out,
    line_in,
    line_sum,
    half_in,
    half_out,
    last_in,
    ksem,
    send_sem,
    recv_sem,
):
    slots, _, panels, width = k_hbm.shape
    clu = w_all.shape[0]
    half = panels // 2
    cols = width // 2
    g = lax.axis_index("grp")
    c = lax.axis_index("clu")
    y, x = c // SIDE, c % SIDE
    has_up, has_down = g < groups - 1, g > 0
    up = {"grp": jnp.minimum(g + 1, groups - 1), "clu": c}
    down = {"grp": jnp.maximum(g - 1, 0), "clu": c}

    def at(a, p, q):
        return q * SIDE + p if a == "x" else p * SIDE + q

    place = {"x": (x, y), "y": (y, x)}

    def near(a, step):
        p, q = place[a]
        return {"grp": g, "clu": at(a, (p + step) % SIDE, q)}

    parts = ksem.shape[0]
    share = slots // parts
    kcopies = [
        pltpu.make_async_copy(
            k_hbm.at[pl.ds(i * share, share)], kbuf.at[pl.ds(i * share, share)], ksem.at[i]
        )
        for i in range(parts)
    ]
    for copy in kcopies:
        copy.start()
    w_all[c] = jnp.transpose(w_ref[...].astype(jnp.float32)).astype(jnp.bfloat16)
    s_all[clu + c] = s_ref[...]

    barrier = pltpu.get_barrier_semaphore()
    for a in ("x", "y"):
        for step in (1, 3):
            pl.semaphore_signal(barrier, inc=1, device_id=near(a, step), device_id_type=MESH)

    @pl.when(has_up)
    def _():
        pl.semaphore_signal(barrier, inc=1, device_id=up, device_id_type=MESH)

    @pl.when(has_down)
    def _():
        pl.semaphore_signal(barrier, inc=1, device_id=down, device_id_type=MESH)

    pl.semaphore_wait(barrier, 4 + has_up.astype(jnp.int32) + has_down.astype(jnp.int32))

    links = Links(send_sem, recv_sem)
    h0, h1 = pl.ds(0, half), pl.ds(half, half)

    W0, S0, ZS = 0, 20, 40
    sides = ((0, 1, h0), (1, 3, h1))

    def w_at(b):
        return w_all.at[b]

    def s_at(b):
        return s_all.at[clu + b]

    def to_groups(b, place_index):
        links.start(ZS + place_index, s_at(b), s_all.at[b], up, has_up)
        links.start(ZS + 16 + place_index, s_at(b), s_all.at[2 * clu + b], down, has_down)

    flows = (("x", "y", w_at, W0), ("y", "x", s_at, S0))

    def second(a1, a2, ref, base, slot, b):
        for d, step, _ in sides:
            links.start(base + 4 + d * 4 + slot, ref(b), ref(b), near(a2, step))

    for a1, a2, ref, base in flows:
        for d, step, _ in sides:
            links.start(base + d, ref(c), ref(c), near(a1, step))
    for a1, a2, ref, base in flows:
        second(a1, a2, ref, base, 0, c)
    to_groups(c, 0)
    for d, step, part in sides:
        for a1, a2, ref, base in flows:
            p, q = place[a1]
            b = at(a1, (p - step) % SIDE, q)
            links.arrived(base + d, ref(b), near(a1, step))
            links.start(base + 2 + d, ref(b).at[part], ref(b).at[part], near(a1, step))
            second(a1, a2, ref, base, 1 + d, b)
            if a1 == "y":
                to_groups(b, 1 + d)
    for a1, a2, ref, base in flows:
        p, q = place[a1]
        b = at(a1, (p + 2) % SIDE, q)
        for d, step, part in sides:
            links.arrived(base + 2 + d, ref(b).at[part], near(a1, step))
        second(a1, a2, ref, base, 3, b)
        if a1 == "y":
            to_groups(b, 3)
    order = (0, 3, 1, 2)
    for slot in range(4):
        for d, step, part in sides:
            for a1, a2, ref, base in flows:
                p, q = place[a1]
                b = at(a1, (p + order[slot]) % SIDE, (q - step) % SIDE)
                links.arrived(base + 4 + d * 4 + slot, ref(b), near(a2, step))
                links.start(base + 12 + d * 4 + slot, ref(b).at[part], ref(b).at[part], near(a2, step))
                if a1 == "y":
                    to_groups(b, 4 + slot * 2 + d)
    for slot in range(4):
        for a1, a2, ref, base in flows:
            p, q = place[a1]
            b = at(a1, (p + order[slot]) % SIDE, (q + 2) % SIDE)
            for d, step, part in sides:
                links.arrived(base + 12 + d * 4 + slot, ref(b).at[part], near(a2, step))
            if a1 == "y":
                to_groups(b, 12 + slot)

    def widen_w(t, carry):
        block = w_all[t]
        w_two[t, :, pl.ds(0, panels)] = block
        w_two[t, :, pl.ds(panels, panels)] = jnp.concatenate([-block[cols:], block[:cols]], axis=0)
        return carry

    lax.fori_loop(0, clu, widen_w, 0)
    for copy in kcopies:
        copy.wait()

    def sums(row, product):
        def body(i, carry):
            total, last = carry
            for u in range(UNROLL):
                k = i * UNROLL + u
                code = tab_ref[row, k]
                mine = code >> 16
                keep = (mine == last).astype(jnp.float32)
                total = total * keep + product(code & 255, (code >> 8) & 255)
                run_buf[k] = total
                last = mine
            return total, last

        lax.fori_loop(
            0, slots // UNROLL, body, (jnp.zeros((panels, width), jnp.float32), jnp.int32(-1))
        )

    def pick(row, out, count):
        def body(b, carry):
            end = tab_ref[row, slots + b]
            begin = tab_ref[row, slots + jnp.maximum(b - 1, 0)] * (b > 0).astype(jnp.int32)
            some = (end > begin).astype(jnp.float32)
            out[b] = run_buf[jnp.maximum(end - 1, 0)] * some
            return carry

        lax.fori_loop(0, count, body, 0)

    def adjoint_product(n, t):
        return jnp.dot(
            w_two[t], kbuf[n].reshape(2 * panels, panels), preferred_element_type=jnp.float32
        )

    sums(1, adjoint_product)
    pick(1, padj, 3 * clu)

    ZA = 72
    ay, aq = place["y"]
    zorder = [at("y", (ay + i) % SIDE, (aq + REL[j]) % SIDE) for i in REL for j in range(4)]
    for i, b in enumerate(zorder):
        links.start(ZA + i, padj.at[2 * clu + b], zin.at[0, b], up, has_up)
        links.start(ZA + 16 + i, padj.at[b], zin.at[1, b], down, has_down)

    gorder = [c]
    yp, yq = place["y"]
    gorder += [at("y", (yp - 1) % SIDE, yq), at("y", (yp + 1) % SIDE, yq), at("y", (yp + 2) % SIDE, yq)]
    for slot in range(4):
        for _, step, _ in sides:
            gorder.append(at("y", (yp + order[slot]) % SIDE, (yq - step) % SIDE))
    for slot in range(4):
        gorder.append(at("y", (yp + order[slot]) % SIDE, (yq + 2) % SIDE))

    lane = lax.broadcasted_iota(jnp.int32, (panels, width), 1)
    sign = jnp.where(lane < cols, -1.0, 1.0).astype(jnp.float32)

    def widen_s(b, carry):
        block = s_all[b]
        s_two[b, pl.ds(0, panels)] = block
        turned = pltpu.roll(block.astype(jnp.float32), cols, 1) * sign
        s_two[b, pl.ds(panels, panels)] = turned.astype(jnp.bfloat16)
        return carry

    def no_s(b, carry):
        s_two[b] = jnp.zeros((2 * panels, width), jnp.bfloat16)
        return carry

    lax.fori_loop(clu, 2 * clu, widen_s, 0)

    @pl.when(has_down)
    def _():
        for i, b in enumerate(gorder):
            links.arrived(ZS + i, s_all.at[b], down)
        lax.fori_loop(0, clu, widen_s, 0)

    @pl.when(jnp.logical_not(has_down))
    def _():
        lax.fori_loop(0, clu, no_s, 0)

    @pl.when(has_up)
    def _():
        for i, b in enumerate(gorder):
            links.arrived(ZS + 16 + i, s_all.at[2 * clu + b], up)
        lax.fori_loop(2 * clu, 3 * clu, widen_s, 0)

    @pl.when(jnp.logical_not(has_up))
    def _():
        lax.fori_loop(2 * clu, 3 * clu, no_s, 0)

    def forward_product(n, s):
        block = kbuf[n]
        return jnp.dot(
            jnp.concatenate([block[0], block[1]], axis=1), s_two[s], preferred_element_type=jnp.float32
        )

    sums(0, forward_product)
    pick(0, ppot, clu)

    class Plane:
        def __init__(self, which, a1, a2, ref):
            self.w, self.a1, self.a2, self.ref = which, a1, a2, ref
            self.base = 104 + 18 * which
            self.p, self.q = place[a1]

        def block(self, dp, j):
            return self.ref(at(self.a1, (self.p + dp) % SIDE, (self.q + REL[j]) % SIDE))

        def first(self):
            w = self.w
            for j in range(4):
                d = j % 2
                links.start(
                    self.base + j, self.block(2, j), relay_in.at[w, j], near(self.a1, 1 if d == 0 else 3)
                )
            for j in range(4):
                d = 1 - j % 2
                links.start(
                    self.base + 4 + 4 * d + j,
                    self.block(1 if d == 0 else 3, j),
                    line_in.at[w, d, j],
                    near(self.a1, 1 if d == 0 else 3),
                )

        def relay(self):
            w = self.w
            for j in range(4):
                d = j % 2
                step = 1 if d == 0 else 3
                links.arrived(self.base + j, relay_in.at[w, j], near(self.a1, step))
                relay_out[w, j] = self.block(step, j)[...] + relay_in[w, j]
                links.start(
                    self.base + 4 + 4 * d + j, relay_out.at[w, j], line_in.at[w, d, j], near(self.a1, step)
                )

        def total(self):
            w = self.w
            for j in range(4):
                for d in range(2):
                    links.arrived(
                        self.base + 4 + 4 * d + j, line_in.at[w, d, j], near(self.a1, 1 if d == 0 else 3)
                    )
                line_sum[w, j] = self.block(0, j)[...] + line_in[w, 0, j] + line_in[w, 1, j]
                if j == 0:
                    for d, step, part in sides:
                        links.start(
                            self.base + 12 + d, line_sum.at[w, 0, part], half_in.at[w, d], near(self.a2, step)
                        )
                if j == 1:
                    links.start(
                        self.base + 15, line_sum.at[w, 1, h1], last_in.at[w, 0, h1], near(self.a2, 1)
                    )
                if j == 2:
                    links.start(
                        self.base + 16, line_sum.at[w, 2, h0], last_in.at[w, 1, h0], near(self.a2, 3)
                    )

        def relay_last(self):
            w = self.w
            for d, step, part in sides:
                links.arrived(self.base + 12 + d, half_in.at[w, d], near(self.a2, step))
                half_out[w, d] = line_sum[w, 1 + d, part] + half_in[w, d]
                links.start(
                    self.base + (14 if d == 0 else 17),
                    half_out.at[w, d],
                    last_in.at[w, d, part],
                    near(self.a2, step),
                )

        def last(self):
            w = self.w
            for d, step, _ in sides:
                for e, part in ((0, h0), (1, h1)):
                    links.arrived(
                        self.base + 14 + 2 * d + e, last_in.at[w, d, part], near(self.a2, step)
                    )
            return line_sum[w, 3] + last_in[w, 0] + last_in[w, 1]

    pot = Plane(0, "x", "y", lambda b: ppot.at[b])
    adj = Plane(1, "y", "x", lambda b: padj.at[clu + b])
    pot.first()
    pot.relay()
    for i, b in enumerate(zorder):

        @pl.when(has_down)
        def _(i=i, b=b):
            links.arrived(ZA + i, zin.at[0, b], down)
            padj[clu + b] += zin[0, b]

        @pl.when(has_up)
        def _(i=i, b=b):
            links.arrived(ZA + 16 + i, zin.at[1, b], up)
            padj[clu + b] += zin[1, b]

    adj.first()
    pot.total()
    adj.relay()
    pot.relay_last()
    adj.total()
    pot_ref[...] = pot.last()
    adj.relay_last()
    adj_ref[...] = jnp.transpose(adj.last())
    links.finish()


def local(groups, strengths, adjoint_weights, kernels, target_ids, source_ids, live_slots):
    slots, _, panels, _ = kernels.shape
    width = strengths.shape[1]
    clu = lax.axis_size("clu")
    g = lax.axis_index("grp")
    n = jnp.arange(slots, dtype=jnp.int32)
    live = n < live_slots[0]
    target = target_ids - g * clu
    source = source_ids - (g - 1) * clu
    place = jnp.stack([jnp.where(live, target, 3 * clu), jnp.where(live, source, 3 * clu)])
    key = place * 256 + n
    rank = jnp.sum((key[:, None, :] < key[:, :, None]).astype(jnp.int32), axis=2)
    load = place * 65536 + jnp.stack([source, target]) * 256 + n
    hit = rank[:, :, None] == n[None, None, :]
    codes = jnp.sum(jnp.where(hit, load[:, :, None], 0), axis=1)
    bound = (jnp.arange(3 * clu, dtype=jnp.int32) + 1) * 256
    ends = jnp.sum((key[:, None, :] < bound[None, :, None]).astype(jnp.int32), axis=2)
    table = jnp.concatenate([codes, ends], axis=1)
    f32, bf16 = jnp.float32, jnp.bfloat16
    vmem = pl.BlockSpec(memory_space=pltpu.VMEM)
    block = (panels, width)
    copies = 140
    return pl.pallas_call(
        functools.partial(kernel, groups),
        out_shape=(jax.ShapeDtypeStruct(block, f32), jax.ShapeDtypeStruct(block, f32)),
        in_specs=[
            vmem,
            vmem,
            pl.BlockSpec(memory_space=pltpu.SMEM),
            pl.BlockSpec(memory_space=pl.ANY),
        ],
        out_specs=(vmem, vmem),
        scratch_shapes=[
            pltpu.VMEM(kernels.shape, bf16),
            pltpu.VMEM((slots, *block), f32),
            pltpu.VMEM((3 * clu, *block), bf16),
            pltpu.VMEM((3 * clu, 2 * panels, width), bf16),
            pltpu.VMEM((clu, width, panels), bf16),
            pltpu.VMEM((clu, width, 2 * panels), bf16),
            pltpu.VMEM((3 * clu, *block), f32),
            pltpu.VMEM((clu, *block), f32),
            pltpu.VMEM((2, clu, *block), f32),
            pltpu.VMEM((2, 4, *block), f32),
            pltpu.VMEM((2, 4, *block), f32),
            pltpu.VMEM((2, 2, 4, *block), f32),
            pltpu.VMEM((2, 4, *block), f32),
            pltpu.VMEM((2, 2, panels // 2, width), f32),
            pltpu.VMEM((2, 2, panels // 2, width), f32),
            pltpu.VMEM((2, 2, *block), f32),
            pltpu.SemaphoreType.DMA((4,)),
            pltpu.SemaphoreType.DMA((copies,)),
            pltpu.SemaphoreType.DMA((copies,)),
        ],
        compiler_params=pltpu.CompilerParams(
            collective_id=0, has_side_effects=True, vmem_limit_bytes=60 * 1024 * 1024
        ),
    )(strengths, adjoint_weights, table, kernels)


def solution(mesh):
    spec = P(("grp", "clu"))
    rows = P(("grp", "clu"), None)
    return jax.shard_map(
        functools.partial(local, mesh.shape["grp"]),
        mesh=mesh,
        in_specs=(rows, rows, P(("grp", "clu"), None, None, None), spec, spec, spec),
        out_specs=(rows, rows),
        check_vma=False,
    )
```

```python
import functools

import jax
import jax.numpy as jnp
from jax import lax
from jax.experimental import pallas as pl
from jax.experimental.pallas import tpu as pltpu
from jax.sharding import PartitionSpec as P

MESH = pl.DeviceIdType.MESH
SIDE = 4
UNROLL = 16
REL = (2, 1, 3, 0)


class Links:
    def __init__(self, send, recv):
        self.send_sem, self.recv_sem, self.open = send, recv, []

    def make(self, index, src, dst, device):
        return pltpu.make_async_remote_copy(
            src_ref=src,
            dst_ref=dst,
            send_sem=self.send_sem.at[index],
            recv_sem=self.recv_sem.at[index],
            device_id=device,
            device_id_type=MESH,
        )

    def start(self, index, src, dst, device, when=None):
        copy = self.make(index, src, dst, device)
        if when is None:
            copy.start()
        else:
            pl.when(when)(copy.start)
        self.open.append((copy, when))

    def pool(self, index, src, dst, device, when):
        pl.when(when)(self.make(index, src, dst, device).start)

    def done(self, index, src, device, when):
        pl.when(when)(self.make(index, src, src, device).wait_send)

    def arrived(self, index, dst, device):
        self.make(index, dst, dst, device).wait_recv()

    def finish(self):
        for copy, when in self.open:
            if when is None:
                copy.wait_send()
            else:
                pl.when(when)(copy.wait_send)


def kernel(
    groups,
    s_ref,
    w_ref,
    tab_ref,
    k_hbm,
    pot_ref,
    adj_ref,
    kbuf,
    run_buf,
    s_all,
    s_two,
    w_all,
    w_two,
    padj,
    ppot,
    zin,
    line_in,
    line_sum,
    last_in,
    ksem,
    send_sem,
    recv_sem,
):
    slots, _, panels, width = k_hbm.shape
    clu = w_all.shape[0]
    half = panels // 2
    cols = width // 2
    g = lax.axis_index("grp")
    c = lax.axis_index("clu")
    y, x = c // SIDE, c % SIDE
    has_up, has_down = g < groups - 1, g > 0
    up = {"grp": jnp.minimum(g + 1, groups - 1), "clu": c}
    down = {"grp": jnp.maximum(g - 1, 0), "clu": c}

    def at(a, p, q):
        return q * SIDE + p if a == "x" else p * SIDE + q

    place = {"x": (x, y), "y": (y, x)}

    def near(a, step):
        p, q = place[a]
        return {"grp": g, "clu": at(a, (p + step) % SIDE, q)}

    parts = ksem.shape[0]
    share = slots // parts
    kcopies = [
        pltpu.make_async_copy(
            k_hbm.at[pl.ds(i * share, share)], kbuf.at[pl.ds(i * share, share)], ksem.at[i]
        )
        for i in range(parts)
    ]
    for copy in kcopies:
        copy.start()
    w_all[c] = jnp.transpose(w_ref[...].astype(jnp.float32)).astype(jnp.bfloat16)
    s_all[clu + c] = s_ref[...]

    barrier = pltpu.get_barrier_semaphore()
    for a in ("x", "y"):
        for step in (1, 2, 3):
            pl.semaphore_signal(barrier, inc=1, device_id=near(a, step), device_id_type=MESH)

    @pl.when(has_up)
    def _():
        pl.semaphore_signal(barrier, inc=1, device_id=up, device_id_type=MESH)

    @pl.when(has_down)
    def _():
        pl.semaphore_signal(barrier, inc=1, device_id=down, device_id_type=MESH)

    pl.semaphore_wait(barrier, 6 + has_up.astype(jnp.int32) + has_down.astype(jnp.int32))

    links = Links(send_sem, recv_sem)
    h0, h1 = pl.ds(0, half), pl.ds(half, half)
    STEPS = (1, 3, 2)

    class Flow:
        def __init__(self, base, a1, a2, part, ref):
            self.base, self.a1, self.a2, self.part, self.ref = base, a1, a2, part, ref
            self.p, self.q = place[a1]

        def piece(self, dp, dq):
            return at(self.a1, (self.p - dp) % SIDE, (self.q - dq) % SIDE)

        def send(self, index, b, axis, step):
            ref = self.ref(b).at[self.part]
            links.start(self.base + index, ref, ref, near(axis, step))

        def wait(self, index, b, axis, step):
            links.arrived(self.base + index, self.ref(b).at[self.part], near(axis, step))

        def begin(self):
            for i, step in enumerate(STEPS):
                self.send(i, self.piece(0, 0), self.a1, step)

        def spread(self, i):
            if i < 3:
                self.wait(i, self.piece(STEPS[i], 0), self.a1, STEPS[i])
            b = self.piece(STEPS[i] if i < 3 else 0, 0)
            for j, step in enumerate(STEPS):
                self.send(3 + 3 * i + j, b, self.a2, step)
            return b

        def late(self, i, j):
            b = self.piece(STEPS[i] if i < 3 else 0, STEPS[j])
            self.wait(3 + 3 * i + j, b, self.a2, STEPS[j])
            return b

    def w_at(b):
        return w_all.at[b]

    def s_at(b):
        return s_all.at[clu + b]

    w_flows = (Flow(0, "x", "y", h0, w_at), Flow(15, "y", "x", h1, w_at))
    s_flows = (Flow(30, "y", "x", h0, s_at), Flow(45, "x", "y", h1, s_at))
    ZS = 60

    def to_groups(flow, b):
        part = flow.part
        links.pool(ZS, s_at(b).at[part], s_all.at[b, part], up, has_up)
        links.pool(ZS + 1, s_at(b).at[part], s_all.at[2 * clu + b, part], down, has_down)

    for flow in w_flows + s_flows:
        flow.begin()
    for flow in w_flows:
        flow.spread(3)
    for flow in s_flows:
        flow.spread(3)
        to_groups(flow, c)
    for i in range(3):
        for flow in w_flows:
            flow.spread(i)
        for flow in s_flows:
            to_groups(flow, flow.spread(i))
    order = [(i, j) for i in (3, 0, 1, 2) for j in range(3)]
    for i, j in order:
        for flow in w_flows:
            flow.late(i, j)

    def strengths_on(pairs):
        def hook():
            for i, j in pairs:
                for flow in s_flows:
                    to_groups(flow, flow.late(i, j))

        return hook

    def widen_w(t, carry):
        block = w_all[t]
        w_two[t, :, pl.ds(0, panels)] = block
        w_two[t, :, pl.ds(panels, panels)] = jnp.concatenate([-block[cols:], block[:cols]], axis=0)
        return carry

    lax.fori_loop(0, clu, widen_w, 0)
    for copy in kcopies:
        copy.wait()

    def sums(row, product, hooks):
        def body(i, carry):
            total, last = carry
            for u in range(UNROLL):
                k = i * UNROLL + u
                code = tab_ref[row, k]
                mine = code >> 16
                keep = (mine == last).astype(jnp.float32)
                total = total * keep + product(code & 255, (code >> 8) & 255)
                run_buf[k] = total
                last = mine
            return total, last

        trips = slots // UNROLL
        carry = (jnp.zeros((panels, width), jnp.float32), jnp.int32(-1))
        for n, hook in enumerate(hooks):
            carry = lax.fori_loop(
                trips * n // len(hooks), trips * (n + 1) // len(hooks), body, carry
            )
            if hook is not None:
                hook()

    def pick(row, out, begin, count):
        def body(b, carry):
            end = tab_ref[row, slots + b]
            start = tab_ref[row, slots + jnp.maximum(b - 1, 0)] * (b > 0).astype(jnp.int32)
            some = (end > start).astype(jnp.float32)
            out[b] = run_buf[jnp.maximum(end - 1, 0)] * some
            return carry

        lax.fori_loop(begin, begin + count, body, 0)

    def adjoint_product(n, t):
        return jnp.dot(
            w_two[t], kbuf[n].reshape(2 * panels, panels), preferred_element_type=jnp.float32
        )

    sums(1, adjoint_product, (strengths_on(order[:6]), strengths_on(order[6:]), None))

    ZA = 62
    offsets = sorted(
        ((dy, dx) for dy in range(SIDE) for dx in range(SIDE)),
        key=lambda o: (min(REL.index(o[0]), REL.index(o[1])), REL.index(o[0]) + REL.index(o[1])),
    )

    def block_at(o):
        return (y + o[0]) % SIDE * SIDE + (x + o[1]) % SIDE

    pick(1, padj, 2 * clu, clu)
    for i, o in enumerate(offsets):
        b = block_at(o)
        links.start(ZA + i, padj.at[2 * clu + b], zin.at[0, b], up, has_up)
    pick(1, padj, 0, clu)
    for i, o in enumerate(offsets):
        b = block_at(o)
        links.start(ZA + 16 + i, padj.at[b], zin.at[1, b], down, has_down)
    pick(1, padj, clu, clu)

    class Half:
        def __init__(self, which, side, a1, a2, part, ref):
            self.w, self.s, self.a1, self.a2, self.part, self.ref = which, side, a1, a2, part, ref
            self.base = 94 + 30 * which + 15 * side
            self.p, self.q = place[a1]

        def send(self, o):
            dp, dq = (o[1], o[0]) if self.a1 == "x" else o
            if dp == 0:
                return
            i, j = REL.index(dp), REL.index(dq)
            links.start(
                self.base + 4 * i + j,
                self.ref(block_at(o)).at[self.part],
                line_in.at[self.w, self.s, i, j],
                near(self.a1, dp),
            )

        def total(self, j):
            for i in range(3):
                links.arrived(
                    self.base + 4 * i + j, line_in.at[self.w, self.s, i, j], near(self.a1, REL[i])
                )
            b = at(self.a1, self.p, (self.q + REL[j]) % SIDE)
            got = line_in.at[self.w, self.s]
            line_sum[self.w, self.s, j] = self.ref(b)[self.part] + got[0, j] + got[1, j] + got[2, j]
            if j < 3:
                links.start(
                    self.base + 12 + j,
                    line_sum.at[self.w, self.s, j],
                    last_in.at[self.w, self.s, j],
                    near(self.a2, REL[j]),
                )

        def last(self):
            got = last_in.at[self.w, self.s]
            for j in range(3):
                links.arrived(self.base + 12 + j, got.at[j], near(self.a2, REL[j]))
            return line_sum[self.w, self.s, 3] + got[0] + got[1] + got[2]

    def halves(which, ref):
        return (
            Half(which, 0, "x", "y", h0, ref),
            Half(which, 1, "y", "x", h1, ref),
        )

    pots = halves(0, lambda b: ppot.at[b])
    adjs = halves(1, lambda b: padj.at[clu + b])

    def adjoint_on(low, high):
        def hook():
            for i in range(low, high):
                b = block_at(offsets[i])

                @pl.when(has_down)
                def _(i=i, b=b):
                    links.arrived(ZA + i, zin.at[0, b], down)
                    padj[clu + b] += zin[0, b]

                @pl.when(has_up)
                def _(i=i, b=b):
                    links.arrived(ZA + 16 + i, zin.at[1, b], up)
                    padj[clu + b] += zin[1, b]

                for part in adjs:
                    part.send(offsets[i])

        return hook

    lane = lax.broadcasted_iota(jnp.int32, (panels, width), 1)
    sign = jnp.where(lane < cols, -1.0, 1.0).astype(jnp.float32)

    def widen_s(b, carry):
        block = s_all[b]
        s_two[b, pl.ds(0, panels)] = block
        turned = pltpu.roll(block.astype(jnp.float32), cols, 1) * sign
        s_two[b, pl.ds(panels, panels)] = turned.astype(jnp.bfloat16)
        return carry

    def no_s(b, carry):
        s_two[b] = jnp.zeros((2 * panels, width), jnp.bfloat16)
        return carry

    lax.fori_loop(clu, 2 * clu, widen_s, 0)

    @pl.when(has_down)
    def _():
        links.arrived(ZS, s_all.at[pl.ds(0, clu)], down)
        lax.fori_loop(0, clu, widen_s, 0)

    @pl.when(jnp.logical_not(has_down))
    def _():
        lax.fori_loop(0, clu, no_s, 0)

    @pl.when(has_up)
    def _():
        links.arrived(ZS + 1, s_all.at[pl.ds(2 * clu, clu)], up)
        lax.fori_loop(2 * clu, 3 * clu, widen_s, 0)

    @pl.when(jnp.logical_not(has_up))
    def _():
        lax.fori_loop(2 * clu, 3 * clu, no_s, 0)

    def forward_product(n, s):
        block = kbuf[n]
        return jnp.dot(
            jnp.concatenate([block[0], block[1]], axis=1), s_two[s], preferred_element_type=jnp.float32
        )

    sums(0, forward_product, (None, None, adjoint_on(0, 4), None))
    pick(0, ppot, 0, clu)
    for o in offsets:
        for part in pots:
            part.send(o)
    adjoint_on(4, 16)()
    for group in (pots, adjs):
        for j in range(4):
            for part in group:
                part.total(j)
    for part in pots:
        pot_ref[part.part] = part.last()
    adj_ref[...] = jnp.transpose(jnp.concatenate([part.last() for part in adjs], axis=0))
    links.done(ZS, s_all.at[pl.ds(clu, clu)], up, has_up)
    links.done(ZS + 1, s_all.at[pl.ds(clu, clu)], down, has_down)
    links.finish()


def local(groups, strengths, adjoint_weights, kernels, target_ids, source_ids, live_slots):
    slots, _, panels, _ = kernels.shape
    width = strengths.shape[1]
    clu = lax.axis_size("clu")
    g = lax.axis_index("grp")
    n = jnp.arange(slots, dtype=jnp.int32)
    live = n < live_slots[0]
    target = target_ids - g * clu
    source = source_ids - (g - 1) * clu
    place = jnp.stack([jnp.where(live, target, 3 * clu), jnp.where(live, source, 3 * clu)])
    key = place * 256 + n
    rank = jnp.sum((key[:, None, :] < key[:, :, None]).astype(jnp.int32), axis=2)
    load = place * 65536 + jnp.stack([source, target]) * 256 + n
    hit = rank[:, :, None] == n[None, None, :]
    codes = jnp.sum(jnp.where(hit, load[:, :, None], 0), axis=1)
    bound = (jnp.arange(3 * clu, dtype=jnp.int32) + 1) * 256
    ends = jnp.sum((key[:, None, :] < bound[None, :, None]).astype(jnp.int32), axis=2)
    table = jnp.concatenate([codes, ends], axis=1)
    f32, bf16 = jnp.float32, jnp.bfloat16
    vmem = pl.BlockSpec(memory_space=pltpu.VMEM)
    block = (panels, width)
    copies = 154
    return pl.pallas_call(
        functools.partial(kernel, groups),
        out_shape=(jax.ShapeDtypeStruct(block, f32), jax.ShapeDtypeStruct(block, f32)),
        in_specs=[
            vmem,
            vmem,
            pl.BlockSpec(memory_space=pltpu.SMEM),
            pl.BlockSpec(memory_space=pl.ANY),
        ],
        out_specs=(vmem, vmem),
        scratch_shapes=[
            pltpu.VMEM(kernels.shape, bf16),
            pltpu.VMEM((slots, *block), f32),
            pltpu.VMEM((3 * clu, *block), bf16),
            pltpu.VMEM((3 * clu, 2 * panels, width), bf16),
            pltpu.VMEM((clu, width, panels), bf16),
            pltpu.VMEM((clu, width, 2 * panels), bf16),
            pltpu.VMEM((3 * clu, *block), f32),
            pltpu.VMEM((clu, *block), f32),
            pltpu.VMEM((2, clu, *block), f32),
            pltpu.VMEM((2, 2, 3, 4, panels // 2, width), f32),
            pltpu.VMEM((2, 2, 4, panels // 2, width), f32),
            pltpu.VMEM((2, 2, 3, panels // 2, width), f32),
            pltpu.SemaphoreType.DMA((4,)),
            pltpu.SemaphoreType.DMA((copies,)),
            pltpu.SemaphoreType.DMA((copies,)),
        ],
        compiler_params=pltpu.CompilerParams(
            collective_id=0, has_side_effects=True, vmem_limit_bytes=60 * 1024 * 1024
        ),
    )(strengths, adjoint_weights, table, kernels)


def solution(mesh):
    spec = P(("grp", "clu"))
    rows = P(("grp", "clu"), None)
    return jax.shard_map(
        functools.partial(local, mesh.shape["grp"]),
        mesh=mesh,
        in_specs=(rows, rows, P(("grp", "clu"), None, None, None), spec, spec, spec),
        out_specs=(rows, rows),
        check_vma=False,
    )
```

```python
import functools

import jax
import jax.numpy as jnp
from jax import lax
from jax.experimental import pallas as pl
from jax.experimental.pallas import tpu as pltpu
from jax.sharding import PartitionSpec as P

MESH = pl.DeviceIdType.MESH
SIDE = 4
UNROLL = 32
REL = (2, 1, 3, 0)


class Links:
    def __init__(self, send, recv):
        self.send_sem, self.recv_sem, self.open = send, recv, []

    def make(self, index, src, dst, device):
        return pltpu.make_async_remote_copy(
            src_ref=src,
            dst_ref=dst,
            send_sem=self.send_sem.at[index],
            recv_sem=self.recv_sem.at[index],
            device_id=device,
            device_id_type=MESH,
        )

    def start(self, index, src, dst, device, when=None):
        copy = self.make(index, src, dst, device)
        if when is None:
            copy.start()
        else:
            pl.when(when)(copy.start)
        self.open.append((copy, when))

    def pool(self, index, src, dst, device, when):
        pl.when(when)(self.make(index, src, dst, device).start)

    def done(self, index, src, device, when):
        pl.when(when)(self.make(index, src, src, device).wait_send)

    def arrived(self, index, dst, device):
        self.make(index, dst, dst, device).wait_recv()

    def finish(self):
        for copy, when in self.open:
            if when is None:
                copy.wait_send()
            else:
                pl.when(when)(copy.wait_send)


def kernel(
    groups,
    s_ref,
    w_ref,
    tab_ref,
    k_hbm,
    out_ref,
    kbuf,
    run_buf,
    s_all,
    s_two,
    w_all,
    w_two,
    padj,
    ppot,
    zin,
    line_in,
    line_sum,
    last_in,
    ksem,
    send_sem,
    recv_sem,
):
    slots, _, panels, width = k_hbm.shape
    clu = w_all.shape[0]
    half = panels // 2
    cols = width // 2
    g = lax.axis_index("grp")
    c = lax.axis_index("clu")
    y, x = c // SIDE, c % SIDE
    has_up, has_down = g < groups - 1, g > 0
    up = {"grp": jnp.minimum(g + 1, groups - 1), "clu": c}
    down = {"grp": jnp.maximum(g - 1, 0), "clu": c}

    def at(a, p, q):
        return q * SIDE + p if a == "x" else p * SIDE + q

    place = {"x": (x, y), "y": (y, x)}

    def near(a, step):
        p, q = place[a]
        return {"grp": g, "clu": at(a, (p + step) % SIDE, q)}

    parts = ksem.shape[0]
    share = slots // parts
    kcopies = [
        pltpu.make_async_copy(
            k_hbm.at[pl.ds(i * share, share)], kbuf.at[pl.ds(i * share, share)], ksem.at[i]
        )
        for i in range(parts)
    ]
    for copy in kcopies:
        copy.start()
    w_all[c] = jnp.transpose(w_ref[...].astype(jnp.float32)).astype(jnp.bfloat16)
    s_all[clu + c] = s_ref[...]

    barrier = pltpu.get_barrier_semaphore()
    for a in ("x", "y"):
        for step in (1, 2, 3):
            pl.semaphore_signal(barrier, inc=1, device_id=near(a, step), device_id_type=MESH)

    @pl.when(has_up)
    def _():
        pl.semaphore_signal(barrier, inc=1, device_id=up, device_id_type=MESH)

    @pl.when(has_down)
    def _():
        pl.semaphore_signal(barrier, inc=1, device_id=down, device_id_type=MESH)

    pl.semaphore_wait(barrier, 6 + has_up.astype(jnp.int32) + has_down.astype(jnp.int32))

    links = Links(send_sem, recv_sem)
    h0, h1 = pl.ds(0, half), pl.ds(half, half)
    STEPS = (1, 3, 2)

    class Flow:
        def __init__(self, base, a1, a2, part, ref):
            self.base, self.a1, self.a2, self.part, self.ref = base, a1, a2, part, ref
            self.p, self.q = place[a1]

        def piece(self, dp, dq):
            return at(self.a1, (self.p - dp) % SIDE, (self.q - dq) % SIDE)

        def send(self, index, b, axis, step):
            ref = self.ref(b).at[self.part]
            links.start(self.base + index, ref, ref, near(axis, step))

        def wait(self, index, b, axis, step):
            links.arrived(self.base + index, self.ref(b).at[self.part], near(axis, step))

        def begin(self):
            for i, step in enumerate(STEPS):
                self.send(i, self.piece(0, 0), self.a1, step)

        def spread(self, i):
            if i < 3:
                self.wait(i, self.piece(STEPS[i], 0), self.a1, STEPS[i])
            b = self.piece(STEPS[i] if i < 3 else 0, 0)
            for j, step in enumerate(STEPS):
                self.send(3 + 3 * i + j, b, self.a2, step)
            return b

        def late(self, i, j):
            b = self.piece(STEPS[i] if i < 3 else 0, STEPS[j])
            self.wait(3 + 3 * i + j, b, self.a2, STEPS[j])
            return b

    def w_at(b):
        return w_all.at[b]

    def s_at(b):
        return s_all.at[clu + b]

    w_flows = (Flow(0, "x", "y", h0, w_at), Flow(15, "y", "x", h1, w_at))
    s_flows = (Flow(30, "y", "x", h0, s_at), Flow(45, "x", "y", h1, s_at))
    ZS = 60

    def to_groups(flow, b):
        part = flow.part
        links.pool(ZS, s_at(b).at[part], s_all.at[b, part], up, has_up)
        links.pool(ZS + 1, s_at(b).at[part], s_all.at[2 * clu + b, part], down, has_down)

    for flow in w_flows + s_flows:
        flow.begin()
    for flow in w_flows:
        flow.spread(3)
    for flow in s_flows:
        flow.spread(3)
        to_groups(flow, c)
    for i in range(3):
        for flow in w_flows:
            flow.spread(i)
        for flow in s_flows:
            to_groups(flow, flow.spread(i))
    order = [(i, j) for i in (3, 0, 1, 2) for j in range(3)]
    for i, j in order:
        for flow in w_flows:
            flow.late(i, j)

    def strengths_on(pairs):
        def hook():
            for i, j in pairs:
                for flow in s_flows:
                    to_groups(flow, flow.late(i, j))

        return hook

    def widen_w(t, carry):
        block = w_all[t]
        w_two[t, :, pl.ds(0, panels)] = block
        w_two[t, :, pl.ds(panels, panels)] = jnp.concatenate([-block[cols:], block[:cols]], axis=0)
        return carry

    lax.fori_loop(0, clu, widen_w, 0)
    for copy in kcopies:
        copy.wait()

    def sums(row, product, hooks):
        def body(i, carry):
            total, last = carry
            for u in range(UNROLL):
                k = i * UNROLL + u
                code = tab_ref[row, k]
                mine = code >> 16
                keep = (mine == last).astype(jnp.float32)
                total = total * keep + product(code & 255, (code >> 8) & 255)
                run_buf[k] = total
                last = mine
            return total, last

        trips = slots // UNROLL
        carry = (jnp.zeros((panels, width), jnp.float32), jnp.int32(-1))
        for n, hook in enumerate(hooks):
            carry = lax.fori_loop(
                trips * n // len(hooks), trips * (n + 1) // len(hooks), body, carry
            )
            if hook is not None:
                hook()

    def pick(row, out, begin, count):
        def body(b, carry):
            end = tab_ref[row, slots + b]
            start = tab_ref[row, slots + jnp.maximum(b - 1, 0)] * (b > 0).astype(jnp.int32)
            some = (end > start).astype(jnp.float32)
            out[b] = run_buf[jnp.maximum(end - 1, 0)] * some
            return carry

        lax.fori_loop(begin, begin + count, body, 0)

    def adjoint_product(n, t):
        return jnp.dot(
            w_two[t], kbuf[n].reshape(2 * panels, panels), preferred_element_type=jnp.float32
        )

    sums(1, adjoint_product, (strengths_on(order[:6]), strengths_on(order[6:]), None))

    ZA = 62
    offsets = sorted(
        ((dy, dx) for dy in range(SIDE) for dx in range(SIDE)),
        key=lambda o: (min(REL.index(o[0]), REL.index(o[1])), REL.index(o[0]) + REL.index(o[1])),
    )

    def block_at(o):
        return (y + o[0]) % SIDE * SIDE + (x + o[1]) % SIDE

    pick(1, padj, 2 * clu, clu)
    for i, o in enumerate(offsets):
        b = block_at(o)
        links.start(ZA + i, padj.at[2 * clu + b], zin.at[0, b], up, has_up)
    pick(1, padj, 0, clu)
    for i, o in enumerate(offsets):
        b = block_at(o)
        links.start(ZA + 16 + i, padj.at[b], zin.at[1, b], down, has_down)
    pick(1, padj, clu, clu)

    class Half:
        def __init__(self, which, side, a1, a2, part, ref):
            self.w, self.s, self.a1, self.a2, self.part, self.ref = which, side, a1, a2, part, ref
            self.base = 94 + 30 * which + 15 * side
            self.p, self.q = place[a1]

        def send(self, o):
            dp, dq = (o[1], o[0]) if self.a1 == "x" else o
            if dp == 0:
                return
            i, j = REL.index(dp), REL.index(dq)
            links.start(
                self.base + 4 * i + j,
                self.ref(block_at(o)).at[self.part],
                line_in.at[self.w, self.s, i, j],
                near(self.a1, dp),
            )

        def total(self, j):
            for i in range(3):
                links.arrived(
                    self.base + 4 * i + j, line_in.at[self.w, self.s, i, j], near(self.a1, REL[i])
                )
            b = at(self.a1, self.p, (self.q + REL[j]) % SIDE)
            got = line_in.at[self.w, self.s]
            line_sum[self.w, self.s, j] = self.ref(b)[self.part] + got[0, j] + got[1, j] + got[2, j]
            if j < 3:
                links.start(
                    self.base + 12 + j,
                    line_sum.at[self.w, self.s, j],
                    last_in.at[self.w, self.s, j],
                    near(self.a2, REL[j]),
                )

        def last(self):
            got = last_in.at[self.w, self.s]
            for j in range(3):
                links.arrived(self.base + 12 + j, got.at[j], near(self.a2, REL[j]))
            return line_sum[self.w, self.s, 3] + got[0] + got[1] + got[2]

    def halves(which, ref):
        return (
            Half(which, 0, "x", "y", h0, ref),
            Half(which, 1, "y", "x", h1, ref),
        )

    pots = halves(0, lambda b: ppot.at[b])
    adjs = halves(1, lambda b: padj.at[clu + b])

    def adjoint_on(low, high):
        def hook():
            for i in range(low, high):
                b = block_at(offsets[i])

                @pl.when(has_down)
                def _(i=i, b=b):
                    links.arrived(ZA + i, zin.at[0, b], down)
                    padj[clu + b] += zin[0, b]

                @pl.when(has_up)
                def _(i=i, b=b):
                    links.arrived(ZA + 16 + i, zin.at[1, b], up)
                    padj[clu + b] += zin[1, b]

                for part in adjs:
                    part.send(offsets[i])

        return hook

    lane = lax.broadcasted_iota(jnp.int32, (panels, width), 1)
    sign = jnp.where(lane < cols, -1.0, 1.0).astype(jnp.float32)

    def widen_s(b, carry):
        block = s_all[b]
        s_two[b, pl.ds(0, panels)] = block
        turned = pltpu.roll(block.astype(jnp.float32), cols, 1) * sign
        s_two[b, pl.ds(panels, panels)] = turned.astype(jnp.bfloat16)
        return carry

    def no_s(b, carry):
        s_two[b] = jnp.zeros((2 * panels, width), jnp.bfloat16)
        return carry

    lax.fori_loop(clu, 2 * clu, widen_s, 0)

    @pl.when(has_down)
    def _():
        links.arrived(ZS, s_all.at[pl.ds(0, clu)], down)
        lax.fori_loop(0, clu, widen_s, 0)

    @pl.when(jnp.logical_not(has_down))
    def _():
        lax.fori_loop(0, clu, no_s, 0)

    @pl.when(has_up)
    def _():
        links.arrived(ZS + 1, s_all.at[pl.ds(2 * clu, clu)], up)
        lax.fori_loop(2 * clu, 3 * clu, widen_s, 0)

    @pl.when(jnp.logical_not(has_up))
    def _():
        lax.fori_loop(2 * clu, 3 * clu, no_s, 0)

    def forward_product(n, s):
        block = kbuf[n]
        return jnp.dot(
            jnp.concatenate([block[0], block[1]], axis=1), s_two[s], preferred_element_type=jnp.float32
        )

    sums(0, forward_product, (None, None, adjoint_on(0, 4), None))
    pick(0, ppot, 0, clu)
    for o in offsets:
        for part in pots:
            part.send(o)
    adjoint_on(4, 16)()
    for group in (pots, adjs):
        for j in range(4):
            for part in group:
                part.total(j)
    for part in pots:
        out_ref[0, part.part] = part.last()
    out_ref[1] = jnp.transpose(jnp.concatenate([part.last() for part in adjs], axis=0))
    links.done(ZS, s_all.at[pl.ds(clu, clu)], up, has_up)
    links.done(ZS + 1, s_all.at[pl.ds(clu, clu)], down, has_down)
    links.finish()


def local(groups, strengths, adjoint_weights, kernels, target_ids, source_ids, live_slots):
    slots, _, panels, _ = kernels.shape
    width = strengths.shape[1]
    clu = lax.axis_size("clu")
    g = lax.axis_index("grp")
    n = jnp.arange(slots, dtype=jnp.int32)
    live = n < live_slots[0]
    target = target_ids - g * clu
    source = source_ids - (g - 1) * clu
    place = jnp.stack([jnp.where(live, target, 3 * clu), jnp.where(live, source, 3 * clu)])
    key = place * 256 + n
    rank = jnp.sum((key[:, None, :] < key[:, :, None]).astype(jnp.int32), axis=2)
    load = place * 65536 + jnp.stack([source, target]) * 256 + n
    hit = rank[:, :, None] == n[None, None, :]
    codes = jnp.sum(jnp.where(hit, load[:, :, None], 0), axis=1)
    bound = (jnp.arange(3 * clu, dtype=jnp.int32) + 1) * 256
    ends = jnp.sum((key[:, None, :] < bound[None, :, None]).astype(jnp.int32), axis=2)
    table = jnp.concatenate([codes, ends], axis=1)
    f32, bf16 = jnp.float32, jnp.bfloat16
    vmem = pl.BlockSpec(memory_space=pltpu.VMEM)
    block = (panels, width)
    copies = 154
    both = pl.pallas_call(
        functools.partial(kernel, groups),
        out_shape=pltpu.VMEM((2, *block), f32),
        in_specs=[
            vmem,
            vmem,
            pl.BlockSpec(memory_space=pltpu.SMEM),
            pl.BlockSpec(memory_space=pl.ANY),
        ],
        out_specs=vmem,
        scratch_shapes=[
            pltpu.VMEM(kernels.shape, bf16),
            pltpu.VMEM((slots, *block), f32),
            pltpu.VMEM((3 * clu, *block), bf16),
            pltpu.VMEM((3 * clu, 2 * panels, width), bf16),
            pltpu.VMEM((clu, width, panels), bf16),
            pltpu.VMEM((clu, width, 2 * panels), bf16),
            pltpu.VMEM((3 * clu, *block), f32),
            pltpu.VMEM((clu, *block), f32),
            pltpu.VMEM((2, clu, *block), f32),
            pltpu.VMEM((2, 2, 3, 4, panels // 2, width), f32),
            pltpu.VMEM((2, 2, 4, panels // 2, width), f32),
            pltpu.VMEM((2, 2, 3, panels // 2, width), f32),
            pltpu.SemaphoreType.DMA((4,)),
            pltpu.SemaphoreType.DMA((copies,)),
            pltpu.SemaphoreType.DMA((copies,)),
        ],
        compiler_params=pltpu.CompilerParams(
            collective_id=0, has_side_effects=True, vmem_limit_bytes=60 * 1024 * 1024
        ),
    )(strengths, adjoint_weights, table, kernels)
    return both[0], both[1]


def solution(mesh):
    spec = P(("grp", "clu"))
    rows = P(("grp", "clu"), None)
    return jax.shard_map(
        functools.partial(local, mesh.shape["grp"]),
        mesh=mesh,
        in_specs=(rows, rows, P(("grp", "clu"), None, None, None), spec, spec, spec),
        out_specs=(rows, rows),
        check_vma=False,
    )
```

```python
import functools

import jax
import jax.numpy as jnp
from jax import lax
from jax.experimental import pallas as pl
from jax.experimental.pallas import tpu as pltpu
from jax.sharding import PartitionSpec as P

MESH = pl.DeviceIdType.MESH
SIDE = 4
UNROLL = 32
REL = (2, 1, 3, 0)


class Links:
    def __init__(self, send, recv):
        self.send_sem, self.recv_sem, self.open = send, recv, []

    def make(self, index, src, dst, device):
        return pltpu.make_async_remote_copy(
            src_ref=src,
            dst_ref=dst,
            send_sem=self.send_sem.at[index],
            recv_sem=self.recv_sem.at[index],
            device_id=device,
            device_id_type=MESH,
        )

    def start(self, index, src, dst, device, when=None):
        copy = self.make(index, src, dst, device)
        if when is None:
            copy.start()
        else:
            pl.when(when)(copy.start)
        self.open.append((copy, when))

    def pool(self, index, src, dst, device, when):
        pl.when(when)(self.make(index, src, dst, device).start)

    def done(self, index, src, device, when):
        pl.when(when)(self.make(index, src, src, device).wait_send)

    def arrived(self, index, dst, device):
        self.make(index, dst, dst, device).wait_recv()

    def finish(self):
        for copy, when in self.open:
            if when is None:
                copy.wait_send()
            else:
                pl.when(when)(copy.wait_send)


def kernel(
    groups,
    s_ref,
    w_ref,
    ids_ref,
    live_ref,
    k_hbm,
    out_ref,
    kbuf,
    run_buf,
    s_all,
    s_two,
    w_all,
    w_two,
    padj,
    ppot,
    zin,
    line_in,
    line_sum,
    last_in,
    rows,
    codes,
    tab_ref,
    tab_sem,
    ksem,
    send_sem,
    recv_sem,
):
    slots, _, panels, width = k_hbm.shape
    clu = w_all.shape[0]
    half = panels // 2
    cols = width // 2
    g = lax.axis_index("grp")
    c = lax.axis_index("clu")
    y, x = c // SIDE, c % SIDE
    has_up, has_down = g < groups - 1, g > 0
    up = {"grp": jnp.minimum(g + 1, groups - 1), "clu": c}
    down = {"grp": jnp.maximum(g - 1, 0), "clu": c}

    def at(a, p, q):
        return q * SIDE + p if a == "x" else p * SIDE + q

    place = {"x": (x, y), "y": (y, x)}

    def near(a, step):
        p, q = place[a]
        return {"grp": g, "clu": at(a, (p + step) % SIDE, q)}

    barrier = pltpu.get_barrier_semaphore()
    for a in ("x", "y"):
        for step in (1, 2, 3):
            pl.semaphore_signal(barrier, inc=1, device_id=near(a, step), device_id_type=MESH)

    @pl.when(has_up)
    def _():
        pl.semaphore_signal(barrier, inc=1, device_id=up, device_id_type=MESH)

    @pl.when(has_down)
    def _():
        pl.semaphore_signal(barrier, inc=1, device_id=down, device_id_type=MESH)

    parts = ksem.shape[0]
    share = slots // parts
    kcopies = [
        pltpu.make_async_copy(
            k_hbm.at[pl.ds(i * share, share)], kbuf.at[pl.ds(i * share, share)], ksem.at[i]
        )
        for i in range(parts)
    ]
    for copy in kcopies:
        copy.start()
    w_all[c] = jnp.transpose(w_ref[...].astype(jnp.float32)).astype(jnp.bfloat16)
    s_all[clu + c] = s_ref[...]

    links = Links(send_sem, recv_sem)
    h0, h1 = pl.ds(0, half), pl.ds(half, half)
    STEPS = (1, 3, 2)

    def tables():
        span = rows.shape[1]
        number = lax.broadcasted_iota(jnp.int32, (1, span), 1)
        live = number < live_ref[0]
        rows[...] = jnp.zeros_like(rows)
        rows[pl.ds(0, 2), pl.ds(0, slots)] = ids_ref[...]
        across = lax.broadcasted_iota(jnp.int32, (span, span), 1)
        down = lambda row: jnp.transpose(jnp.broadcast_to(row, (span, span)))
        locals_ = [
            jnp.clip(rows[pl.ds(0, 1)] - g * clu, 0, clu - 1),
            jnp.clip(rows[pl.ds(1, 1)] - (g - 1) * clu, 0, 3 * clu - 1),
        ]
        for i in range(2):
            spot = jnp.where(live, locals_[i], 3 * clu)
            key = spot * 256 + number
            key_down = down(key)
            rank = jnp.sum((key_down < key).astype(jnp.int32), axis=0, keepdims=True)
            load = down(spot * 65536 + locals_[1 - i] * 256 + number)
            codes[pl.ds(i, 1)] = jnp.sum(jnp.where(down(rank) == across, load, 0), axis=0, keepdims=True)
            ends = (key_down < (across + 1) * 256).astype(jnp.int32)
            codes[pl.ds(2 + i, 1)] = jnp.sum(ends, axis=0, keepdims=True)
        copy = pltpu.make_async_copy(codes, tab_ref, tab_sem)
        copy.start()
        return copy

    table_copy = tables()
    pl.semaphore_wait(barrier, 6 + has_up.astype(jnp.int32) + has_down.astype(jnp.int32))

    class Flow:
        def __init__(self, base, a1, a2, part, ref):
            self.base, self.a1, self.a2, self.part, self.ref = base, a1, a2, part, ref
            self.p, self.q = place[a1]

        def piece(self, dp, dq):
            return at(self.a1, (self.p - dp) % SIDE, (self.q - dq) % SIDE)

        def send(self, index, b, axis, step):
            ref = self.ref(b).at[self.part]
            links.start(self.base + index, ref, ref, near(axis, step))

        def wait(self, index, b, axis, step):
            links.arrived(self.base + index, self.ref(b).at[self.part], near(axis, step))

        def begin(self):
            for i, step in enumerate(STEPS):
                self.send(i, self.piece(0, 0), self.a1, step)

        def spread(self, i):
            if i < 3:
                self.wait(i, self.piece(STEPS[i], 0), self.a1, STEPS[i])
            b = self.piece(STEPS[i] if i < 3 else 0, 0)
            for j, step in enumerate(STEPS):
                self.send(3 + 3 * i + j, b, self.a2, step)
            return b

        def late(self, i, j):
            b = self.piece(STEPS[i] if i < 3 else 0, STEPS[j])
            self.wait(3 + 3 * i + j, b, self.a2, STEPS[j])
            return b

    def w_at(b):
        return w_all.at[b]

    def s_at(b):
        return s_all.at[clu + b]

    w_flows = (Flow(0, "x", "y", h0, w_at), Flow(15, "y", "x", h1, w_at))
    s_flows = (Flow(30, "y", "x", h0, s_at), Flow(45, "x", "y", h1, s_at))
    ZS = 60

    def to_groups(flow, b):
        part = flow.part
        links.pool(ZS, s_at(b).at[part], s_all.at[b, part], up, has_up)
        links.pool(ZS + 1, s_at(b).at[part], s_all.at[2 * clu + b, part], down, has_down)

    for flow in w_flows + s_flows:
        flow.begin()
    for flow in w_flows:
        flow.spread(3)
    for flow in s_flows:
        flow.spread(3)
        to_groups(flow, c)
    for i in range(3):
        for flow in w_flows:
            flow.spread(i)
        for flow in s_flows:
            to_groups(flow, flow.spread(i))
    order = [(i, j) for i in (3, 0, 1, 2) for j in range(3)]
    for i, j in order:
        for flow in w_flows:
            flow.late(i, j)

    def strengths_on(pairs):
        def hook():
            for i, j in pairs:
                for flow in s_flows:
                    to_groups(flow, flow.late(i, j))

        return hook

    def widen_w(t, carry):
        block = w_all[t]
        w_two[t, :, pl.ds(0, panels)] = block
        w_two[t, :, pl.ds(panels, panels)] = jnp.concatenate([-block[cols:], block[:cols]], axis=0)
        return carry

    lax.fori_loop(0, clu, widen_w, 0)
    for copy in kcopies:
        copy.wait()
    table_copy.wait()

    def sums(row, product, hooks):
        def body(i, carry):
            total, last = carry
            for u in range(UNROLL):
                k = i * UNROLL + u
                code = tab_ref[row, k]
                mine = code >> 16
                keep = (mine == last).astype(jnp.float32)
                total = total * keep + product(code & 255, (code >> 8) & 255)
                run_buf[k] = total
                last = mine
            return total, last

        trips = slots // UNROLL
        carry = (jnp.zeros((panels, width), jnp.float32), jnp.int32(-1))
        for n, hook in enumerate(hooks):
            carry = lax.fori_loop(
                trips * n // len(hooks), trips * (n + 1) // len(hooks), body, carry
            )
            if hook is not None:
                hook()

    def pick(row, out, begin, count):
        def body(b, carry):
            end = tab_ref[2 + row, b]
            start = tab_ref[2 + row, jnp.maximum(b - 1, 0)] * (b > 0).astype(jnp.int32)
            some = (end > start).astype(jnp.float32)
            out[b] = run_buf[jnp.maximum(end - 1, 0)] * some
            return carry

        lax.fori_loop(begin, begin + count, body, 0)

    def adjoint_product(n, t):
        return jnp.dot(
            w_two[t], kbuf[n].reshape(2 * panels, panels), preferred_element_type=jnp.float32
        )

    sums(1, adjoint_product, (strengths_on(order[:6]), strengths_on(order[6:]), None))

    ZA = 62
    offsets = sorted(
        ((dy, dx) for dy in range(SIDE) for dx in range(SIDE)),
        key=lambda o: (min(REL.index(o[0]), REL.index(o[1])), REL.index(o[0]) + REL.index(o[1])),
    )

    def block_at(o):
        return (y + o[0]) % SIDE * SIDE + (x + o[1]) % SIDE

    pick(1, padj, 2 * clu, clu)
    for i, o in enumerate(offsets):
        b = block_at(o)
        links.start(ZA + i, padj.at[2 * clu + b], zin.at[0, b], up, has_up)
    pick(1, padj, 0, clu)
    for i, o in enumerate(offsets):
        b = block_at(o)
        links.start(ZA + 16 + i, padj.at[b], zin.at[1, b], down, has_down)
    pick(1, padj, clu, clu)

    class Half:
        def __init__(self, which, side, a1, a2, part, ref):
            self.w, self.s, self.a1, self.a2, self.part, self.ref = which, side, a1, a2, part, ref
            self.base = 94 + 30 * which + 15 * side
            self.p, self.q = place[a1]

        def send(self, o):
            dp, dq = (o[1], o[0]) if self.a1 == "x" else o
            if dp == 0:
                return
            i, j = REL.index(dp), REL.index(dq)
            links.start(
                self.base + 4 * i + j,
                self.ref(block_at(o)).at[self.part],
                line_in.at[self.w, self.s, i, j],
                near(self.a1, dp),
            )

        def total(self, j):
            for i in range(3):
                links.arrived(
                    self.base + 4 * i + j, line_in.at[self.w, self.s, i, j], near(self.a1, REL[i])
                )
            b = at(self.a1, self.p, (self.q + REL[j]) % SIDE)
            got = line_in.at[self.w, self.s]
            line_sum[self.w, self.s, j] = self.ref(b)[self.part] + got[0, j] + got[1, j] + got[2, j]
            if j < 3:
                links.start(
                    self.base + 12 + j,
                    line_sum.at[self.w, self.s, j],
                    last_in.at[self.w, self.s, j],
                    near(self.a2, REL[j]),
                )

        def last(self):
            got = last_in.at[self.w, self.s]
            for j in range(3):
                links.arrived(self.base + 12 + j, got.at[j], near(self.a2, REL[j]))
            return line_sum[self.w, self.s, 3] + got[0] + got[1] + got[2]

    def halves(which, ref):
        return (
            Half(which, 0, "x", "y", h0, ref),
            Half(which, 1, "y", "x", h1, ref),
        )

    pots = halves(0, lambda b: ppot.at[b])
    adjs = halves(1, lambda b: padj.at[clu + b])

    def adjoint_on(low, high):
        def hook():
            for i in range(low, high):
                b = block_at(offsets[i])

                @pl.when(has_down)
                def _(i=i, b=b):
                    links.arrived(ZA + i, zin.at[0, b], down)
                    padj[clu + b] += zin[0, b]

                @pl.when(has_up)
                def _(i=i, b=b):
                    links.arrived(ZA + 16 + i, zin.at[1, b], up)
                    padj[clu + b] += zin[1, b]

                for part in adjs:
                    part.send(offsets[i])

        return hook

    lane = lax.broadcasted_iota(jnp.int32, (panels, width), 1)
    sign = jnp.where(lane < cols, -1.0, 1.0).astype(jnp.float32)

    def widen_s(b, carry):
        block = s_all[b]
        s_two[b, pl.ds(0, panels)] = block
        turned = pltpu.roll(block.astype(jnp.float32), cols, 1) * sign
        s_two[b, pl.ds(panels, panels)] = turned.astype(jnp.bfloat16)
        return carry

    def no_s(b, carry):
        s_two[b] = jnp.zeros((2 * panels, width), jnp.bfloat16)
        return carry

    lax.fori_loop(clu, 2 * clu, widen_s, 0)

    @pl.when(has_down)
    def _():
        links.arrived(ZS, s_all.at[pl.ds(0, clu)], down)
        lax.fori_loop(0, clu, widen_s, 0)

    @pl.when(jnp.logical_not(has_down))
    def _():
        lax.fori_loop(0, clu, no_s, 0)

    @pl.when(has_up)
    def _():
        links.arrived(ZS + 1, s_all.at[pl.ds(2 * clu, clu)], up)
        lax.fori_loop(2 * clu, 3 * clu, widen_s, 0)

    @pl.when(jnp.logical_not(has_up))
    def _():
        lax.fori_loop(2 * clu, 3 * clu, no_s, 0)

    def forward_product(n, s):
        block = kbuf[n]
        return jnp.dot(
            jnp.concatenate([block[0], block[1]], axis=1), s_two[s], preferred_element_type=jnp.float32
        )

    sums(
        0,
        forward_product,
        (None, None, adjoint_on(0, 3), adjoint_on(3, 5), adjoint_on(5, 7), adjoint_on(7, 8)),
    )
    pick(0, ppot, 0, clu)
    for o in offsets:
        for part in pots:
            part.send(o)
    adjoint_on(8, 16)()
    for group in (pots, adjs):
        for j in range(4):
            for part in group:
                part.total(j)
    for part in pots:
        out_ref[0, part.part] = part.last()
    out_ref[1] = jnp.transpose(jnp.concatenate([part.last() for part in adjs], axis=0))
    links.done(ZS, s_all.at[pl.ds(clu, clu)], up, has_up)
    links.done(ZS + 1, s_all.at[pl.ds(clu, clu)], down, has_down)
    links.finish()


def local(groups, strengths, adjoint_weights, kernels, target_ids, source_ids, live_slots):
    slots, _, panels, _ = kernels.shape
    width = strengths.shape[1]
    clu = lax.axis_size("clu")
    ids = jnp.stack([target_ids, source_ids])
    span = -(-slots // 128) * 128
    f32, bf16 = jnp.float32, jnp.bfloat16
    vmem = pl.BlockSpec(memory_space=pltpu.VMEM)
    block = (panels, width)
    copies = 154
    both = pl.pallas_call(
        functools.partial(kernel, groups),
        out_shape=pltpu.VMEM((2, *block), f32),
        in_specs=[
            vmem,
            vmem,
            vmem,
            pl.BlockSpec(memory_space=pltpu.SMEM),
            pl.BlockSpec(memory_space=pl.ANY),
        ],
        out_specs=vmem,
        scratch_shapes=[
            pltpu.VMEM(kernels.shape, bf16),
            pltpu.VMEM((slots, *block), f32),
            pltpu.VMEM((3 * clu, *block), bf16),
            pltpu.VMEM((3 * clu, 2 * panels, width), bf16),
            pltpu.VMEM((clu, width, panels), bf16),
            pltpu.VMEM((clu, width, 2 * panels), bf16),
            pltpu.VMEM((3 * clu, *block), f32),
            pltpu.VMEM((clu, *block), f32),
            pltpu.VMEM((2, clu, *block), f32),
            pltpu.VMEM((2, 2, 3, 4, panels // 2, width), f32),
            pltpu.VMEM((2, 2, 4, panels // 2, width), f32),
            pltpu.VMEM((2, 2, 3, panels // 2, width), f32),
            pltpu.VMEM((8, span), jnp.int32),
            pltpu.VMEM((8, span), jnp.int32),
            pltpu.SMEM((8, span), jnp.int32),
            pltpu.SemaphoreType.DMA,
            pltpu.SemaphoreType.DMA((4,)),
            pltpu.SemaphoreType.DMA((copies,)),
            pltpu.SemaphoreType.DMA((copies,)),
        ],
        compiler_params=pltpu.CompilerParams(
            collective_id=0, has_side_effects=True, vmem_limit_bytes=60 * 1024 * 1024
        ),
    )(strengths, adjoint_weights, ids, live_slots, kernels)
    return both[0], both[1]


def solution(mesh):
    spec = P(("grp", "clu"))
    rows = P(("grp", "clu"), None)
    return jax.shard_map(
        functools.partial(local, mesh.shape["grp"]),
        mesh=mesh,
        in_specs=(rows, rows, P(("grp", "clu"), None, None, None), spec, spec, spec),
        out_specs=(rows, rows),
        check_vma=False,
    )
```
